32 devices in a mesh: section: 4 (over y, x), tensor: 8 (over z, core).
Axes of the slice: x: 2, y: 2, z: 4, core: 2. Of those that a mesh axis runs over, the one named last changes fastest.
Arguments:
- hidden_last: bfloat16 [512, 6656], P(None, 'tensor'), may hold values from -6 to 6
- labels: int32 [512], replicated, may hold values from 0 to 31999
- head_weight: bfloat16 [6656, 32000], P(None, 'tensor'), may hold values from -0.21875 to 0.21875
- layer_inputs: bfloat16 [4, 512, 6656], P('section', None, 'tensor'), may hold values from -6 to 6
- weights: bfloat16 [4, 6656, 6656], P('section', 'tensor'), may hold values from -0.078125 to 0.078125
- row_state: float32 [4, 6656], P('section', 'tensor'), may hold values from 1.173753e-06 to 0.000498845
- col_state: float32 [4, 6656], P('section'), may hold values from 1e-08 to 1e-06
Outputs:
- loss: float32 [], replicated
- input_grads: bfloat16 [4, 512, 6656], P('section', None, 'tensor')
- new_weights: bfloat16 [4, 6656, 6656], P('section', 'tensor')
- new_row_state: float32 [4, 6656], P('section', 'tensor')
- new_col_state: float32 [4, 6656], P('section')
The draws below stay inside these ranges and needn't reach their ends.
All inputs are finite; a program needn't handle non-finite values.
Results may differ from the reference program's by a relative error of at most 0.007.
Values may be sent and summed in bfloat16 or wider, within the bound.
A program may use at most 192 MiB of HBM per device.

```python
import math
import jax
import jax.numpy as jnp
from jax import lax

D = 6656
VOCAB = 32000
SECTIONS = 4
TOKENS = 512


def draw_row_state(key, part):
    base_scale = 9.0 / (TOKENS * D)
    end_factor = 30.0
    position = jnp.arange(D, dtype=jnp.float32) / (D - 1)
    rising = jnp.exp(position * math.log(end_factor))
    roughness = jnp.exp(jax.random.uniform(key, (SECTIONS, D), jnp.float32, math.log(0.5), math.log(2.0)))
    return (base_scale * rising[None, :] * roughness).astype(jnp.float32)


def with_ends(result, key, least, largest):
    longest = result.shape.index(max(result.shape))
    spots = []
    for shift in (0, 1):
        where = [jax.random.randint(jax.random.fold_in(key, axis), (), 0, length) for axis, length in enumerate(result.shape)]
        where[longest] = (where[longest] + shift) % result.shape[longest]
        spots.append(tuple(where))
    return result.at[spots[0]].set(least).at[spots[1]].set(largest)


def block_levels(stream_key, shape, cuts, smallest, high):
    factor_of, own = 1.0, jax.random.fold_in(stream_key, 6)
    for dim, shards_of in cuts:
        draws = jnp.exp(jax.random.uniform(jax.random.fold_in(own, dim), (shards_of,), jnp.float32, smallest / len(cuts), high / len(cuts)))
        factor_of = factor_of * jnp.repeat(draws, shape[dim] // shards_of).reshape([-1 if axis == dim else 1 for axis in range(len(shape))])
    return factor_of


def scatter_about(stream_key, dims, deviation, limit, shards=(), kind=jnp.bfloat16):
    gain = block_levels(stream_key, dims, shards, -0.22, 0.18) if shards else 1.0
    drawn = jax.random.normal(stream_key, dims, jnp.float32) * deviation * gain
    return jnp.minimum(jnp.maximum(drawn, -limit), limit).astype(kind)


def setup_inputs(seed: int = 0) -> dict:
    key_of = jax.random.split(jax.random.key(seed), 8)
    return {
        "hidden_last": scatter_about(key_of[0], (TOKENS, D), 1.0, 6.0, ((1, 8),)),
        "labels": with_ends(jax.random.randint(key_of[1], (TOKENS,), 0, VOCAB), jax.random.fold_in(key_of[1], 1), 0, VOCAB - 1).astype(jnp.int32),
        "head_weight": scatter_about(key_of[2], (D, VOCAB), (D // 9) ** -0.5, 0.21875, ((1, 8),)),
        "layer_inputs": scatter_about(key_of[3], (SECTIONS, TOKENS, D), 1.0, 6.0, ((0, 4), (2, 8))),
        "weights": scatter_about(key_of[4], (SECTIONS, D, D), D ** -0.5, 0.078125, ((0, 4), (1, 8))),
        "row_state": draw_row_state(jax.random.fold_in(key_of[7], 71), 0),
        "col_state": jnp.clip(jnp.exp(math.log(9.999999974752427e-07) - 4.6051702 * jax.random.uniform(key_of[6], (SECTIONS, D), jnp.float32) ** block_levels(key_of[6], (SECTIONS, D), ((0, 4),), -0.2, 0.2)), 9.99999993922529e-09, 9.999999974752427e-07),
    }


decay_rate = 0.9
learn_rate = 0.3
tiny_term = 1e-30

def adalomo(gradient, weight, row_prev, col_prev):
    model_width = weight.shape[0]
    squares = gradient * gradient + tiny_term
    row_new = decay_rate * row_prev + (1.0 - decay_rate) * lax.optimization_barrier(jnp.mean(squares, axis=1))
    col_new = decay_rate * col_prev + (1.0 - decay_rate) * lax.optimization_barrier(jnp.mean(squares, axis=0))
    second = row_new[:, None] * col_new[None, :] / jnp.sum(row_new)
    update = gradient / jnp.sqrt(second)
    entries = float(model_width * model_width)
    weight_float = weight.astype(jnp.float32)
    update_rms = jnp.sqrt(jnp.sum(update * update) / entries)
    weight_rms = jnp.sqrt(jnp.sum(weight_float * weight_float) / entries)
    factor = learn_rate * weight_rms / jnp.maximum(1.0, update_rms)
    return ((weight_float - factor * update).astype(jnp.bfloat16), row_new, col_new)

def reference(hidden_last, labels, head_weight, layer_inputs, weights, row_state, col_state):
    all_rows = labels.shape[0]
    logits = jnp.dot(hidden_last, head_weight, preferred_element_type=jnp.float32)
    exponent = jnp.exp(logits)
    label_hit = labels[:, None] == jnp.arange(head_weight.shape[1], dtype=jnp.int32)[None, :]
    denominator = lax.optimization_barrier(jnp.sum(exponent, axis=1))
    picked = lax.optimization_barrier(jnp.sum(jnp.where(label_hit, logits, jnp.zeros_like(logits)), axis=1))
    loss = jnp.sum(jnp.log(denominator) - picked) / all_rows
    logit_grad = ((exponent / denominator[:, None] - label_hit.astype(jnp.float32)) / all_rows).astype(jnp.bfloat16)
    carried = jnp.dot(logit_grad, head_weight.T, preferred_element_type=jnp.float32).astype(jnp.bfloat16)
    grads_list, weight_list, row_list, col_list = ([], [], [], [])
    for layer_index in reversed(range(weights.shape[0])):
        weight = weights[layer_index]
        saved = layer_inputs[layer_index]
        backward = jnp.dot(carried, weight.T, preferred_element_type=jnp.float32)
        input_grad = (carried.astype(jnp.float32) + backward).astype(jnp.bfloat16)
        gradient = jnp.dot(saved.T, carried, preferred_element_type=jnp.float32)
        new_weight, row_new, col_new = adalomo(gradient, weight, row_state[layer_index], col_state[layer_index])
        grads_list.insert(0, input_grad)
        weight_list.insert(0, new_weight)
        row_list.insert(0, row_new)
        col_list.insert(0, col_new)
        carried = input_grad
    return (loss, jnp.stack(grads_list), jnp.stack(weight_list), jnp.stack(row_list), jnp.stack(col_list))
```

```python
import functools

import jax
import jax.numpy as jnp
from jax import lax
from jax.experimental import pallas as pl
from jax.experimental.pallas import tpu as pltpu
from jax.sharding import PartitionSpec as P

decay_rate = 0.9
learn_rate = 0.3
tiny_term = 1e-30


MESH = pl.DeviceIdType.MESH


def chain_kernel(
    sections, tensors, part_ref, loss_ref, w_ref, out_ref, g_ref, total_ref,
    loss_buf, send_x, recv_x, send_ring, recv_ring, send_mate, recv_mate, send_loss, recv_loss, head_sem,
):
    section = lax.axis_index("section")
    me = lax.axis_index("tensor")
    chips = tensors // 2
    chip, core = me // 2, me % 2
    right = lax.rem(chip + 1, chips) * 2 + core
    left = lax.rem(chip + chips - 1, chips) * 2 + core
    mate = chip * 2 + 1 - core
    features, lanes = part_ref.shape
    half = features // 2 // 16 * 16
    last = sections - 1
    reach = chips // 2

    def block(share, origin, low, size):
        rows = pl.ds(pl.multiple_of(origin * features + low, 16), size)
        return g_ref.at[rows, pl.ds(pl.multiple_of(share * lanes, lanes), lanes)]

    def span(way, distance):
        if 2 * distance < chips:
            return 0, features
        return (0, half) if way == 0 else (half, features - half)

    def remote(src, dst, send, recv, device):
        return pltpu.make_async_remote_copy(
            src_ref=src, dst_ref=dst, send_sem=send, recv_sem=recv, device_id=device, device_id_type=MESH
        )

    def origin_of(way, distance):
        there = chip - distance if way == 0 else chip + distance
        return lax.rem(there + chips, chips) * 2 + core

    def ring_copy(share, way, distance, origin):
        low, size = span(way, distance)
        where = block(share, origin, low, size)
        slot = (share, way * reach + distance - 1)
        return remote(
            where, where, send_ring.at[slot], recv_ring.at[slot], {"tensor": right if way == 0 else left}
        )

    def mate_copy(share, way, distance, origin):
        low, size = (0, features) if distance == 0 else span(way, distance)
        where = block(share, origin, low, size)
        slot = (share, 0 if distance == 0 else 1 + way * reach + distance - 1)
        return remote(where, where, send_mate.at[slot], recv_mate.at[slot], {"tensor": mate})

    def down_copy(share):
        columns = pl.ds(pl.multiple_of(share * lanes, lanes), lanes)
        below = jnp.maximum(section - 1, 0)
        return remote(
            out_ref.at[:, columns], block(share, me, 0, features),
            send_x.at[share], recv_x.at[share], {"section": below},
        )

    def head_copy():
        return remote(
            part_ref, block(section, me, 0, features), head_sem.at[0], recv_x.at[section], {"section": last}
        )

    def own_copy():
        return pltpu.make_async_copy(part_ref, block(last, me, 0, features), head_sem.at[1])

    def loss_copy(step):
        other = lax.rem(section + step, sections)
        return remote(
            loss_ref, loss_buf.at[step - 1], send_loss.at[step - 1], recv_loss.at[step - 1], {"section": other}
        )

    barrier = pltpu.get_barrier_semaphore()
    greeted = [{"tensor": mate}]
    if reach:
        greeted += [{"tensor": right}, {"tensor": left}]
    greeted += [{"section": lax.rem(section + step, sections)} for step in range(1, sections)]
    for device in greeted:
        pl.semaphore_signal(barrier, inc=1, device_id=device, device_id_type=MESH)
    pl.semaphore_wait(barrier, len(greeted))

    @pl.when(section == last)
    def _():
        own_copy().start()

    @pl.when(section != last)
    def _():
        head_copy().start()

    for step in range(1, sections):
        loss_copy(step).start()

    tile = features // 2 if features > 416 else features

    def advance(share, carry):
        @pl.when((section == last) & (share == last))
        def _():
            own_copy().wait()

        @pl.when((section != last) | (share != last))
        def _():
            down_copy(share).wait_recv()

        if reach:
            ring_copy(share, 0, 1, me).start()
            ring_copy(share, 1, 1, me).start()
        mate_copy(share, 0, 0, me).start()
        for distance in range(1, reach + 1):
            for way in (0, 1):
                origin = origin_of(way, distance)
                ring_copy(share, way, distance, origin).wait_recv()
                if distance < reach:
                    ring_copy(share, way, distance + 1, origin).start()
                mate_copy(share, way, distance, origin).start()
        other = 1 - 2 * core
        mate_copy(share, 0, 0, me + other).wait_recv()
        for distance in range(1, reach + 1):
            for way in (0, 1):
                mate_copy(share, way, distance, origin_of(way, distance) + other).wait_recv()
        columns = pl.ds(pl.multiple_of(share * lanes, lanes), lanes)

        def rows_step(index, inner):
            rows = pl.ds(pl.multiple_of(index * tile, 16), tile)
            mine = g_ref[pl.ds(pl.multiple_of(me * features + index * tile, 16), tile), columns]
            product = jnp.dot(w_ref[rows, :], g_ref[:, columns], preferred_element_type=jnp.float32)
            out_ref[rows, columns] = (mine.astype(jnp.float32) + product).astype(out_ref.dtype)
            return inner

        lax.fori_loop(0, features // tile, rows_step, 0)

        @pl.when(section > 0)
        def _():
            down_copy(share).start()

        return carry

    lax.fori_loop(0, sections, advance, 0)

    total = loss_ref[...]
    for step in range(1, sections):
        loss_copy(step).wait_recv()
        total = total + loss_buf[step - 1]
    total_ref[...] = total

    def finish(share, carry):
        @pl.when(section > 0)
        def _():
            down_copy(share).wait_send()

        if reach:
            ring_copy(share, 0, 1, me).wait_send()
            ring_copy(share, 1, 1, me).wait_send()
        mate_copy(share, 0, 0, me).wait_send()
        for distance in range(1, reach + 1):
            for way in (0, 1):
                origin = origin_of(way, distance)
                if distance < reach:
                    ring_copy(share, way, distance + 1, origin).wait_send()
                mate_copy(share, way, distance, origin).wait_send()
        return carry

    lax.fori_loop(0, sections, finish, 0)
    for step in range(1, sections):
        loss_copy(step).wait_send()

    @pl.when(section != last)
    def _():
        head_copy().wait_send()


def chain(part_grad, part_loss, local_weight):
    sections, tensors = lax.axis_size("section"), lax.axis_size("tensor")
    features, lanes = part_grad.shape
    width = features * tensors
    rows = lanes * sections
    ring = max(2 * (tensors // 4), 1)
    dma = pltpu.SemaphoreType.DMA
    vmem = pl.BlockSpec(memory_space=pltpu.VMEM)
    return pl.pallas_call(
        functools.partial(chain_kernel, sections, tensors),
        out_shape=(
            jax.ShapeDtypeStruct((features, rows), jnp.bfloat16),
            jax.ShapeDtypeStruct((width, rows), jnp.bfloat16),
            jax.ShapeDtypeStruct((8, 128), jnp.float32),
        ),
        in_specs=[vmem] * 3,
        out_specs=(vmem, vmem, vmem),
        scratch_shapes=[
            pltpu.VMEM((max(sections - 1, 1), 8, 128), jnp.float32),
            dma((sections,)),
            dma((sections,)),
            dma((sections, ring)),
            dma((sections, ring)),
            dma((sections, ring + 1)),
            dma((sections, ring + 1)),
            dma((max(sections - 1, 1),)),
            dma((max(sections - 1, 1),)),
            dma((2,)),
        ],
        compiler_params=pltpu.CompilerParams(
            collective_id=0, has_side_effects=True, vmem_limit_bytes=48 * 1024 * 1024
        ),
    )(part_grad, jnp.full((8, 128), part_loss, jnp.float32), local_weight)


def body(hidden_last, labels, head_weight, layer_inputs, weights, row_state, col_state):
    section_count = lax.axis_size("section")
    section_index = lax.axis_index("section")
    all_rows = labels.shape[0]
    model_width = head_weight.shape[0]
    vocab_local = head_weight.shape[1]
    local_weight = weights[0]
    rows_local = local_weight.shape[0]
    saved_all = layer_inputs[0]
    columns = lax.axis_index("tensor") * vocab_local + lax.iota(jnp.int32, vocab_local)
    share_rows = all_rows // section_count
    row_start = section_index * share_rows
    hidden_rows = lax.dynamic_slice_in_dim(hidden_last, row_start, share_rows, 0)
    head_slice = head_weight
    logits = jnp.dot(
        lax.all_gather(hidden_rows, "tensor", axis=1, tiled=True),
        head_slice,
        preferred_element_type=jnp.float32,
    )
    exponent = jnp.exp(logits)
    label_hit = (
        lax.dynamic_slice_in_dim(labels, row_start, share_rows, 0)[:, None] == columns[None, :]
    )
    denominator, picked = lax.psum(
        (
            jnp.sum(exponent, axis=1),
            jnp.sum(jnp.where(label_hit, logits, jnp.zeros_like(logits)), axis=1),
        ),
        "tensor",
    )
    losses = jnp.log(denominator) - picked
    logit_grad = (
        (exponent / denominator[:, None] - label_hit.astype(jnp.float32)) / all_rows
    ).astype(jnp.bfloat16)
    head_slice = head_weight
    shares = lax.psum_scatter(
        lax.dot_general(
            head_slice, logit_grad, (((1,), (1,)), ((), ())), preferred_element_type=jnp.float32
        ),
        "tensor",
        scatter_dimension=0,
        tiled=True,
    )
    part_grad = shares.astype(jnp.bfloat16)
    part_loss = jnp.sum(losses)
    outputs, gathered, total = chain(part_grad, part_loss, local_weight)
    loss = total[0, 0] / all_rows
    gradient = lax.dot_general(
        saved_all, gathered, (((0,), (1,)), ((), ())), preferred_element_type=jnp.float32
    )
    weight_float = local_weight.astype(jnp.float32)
    entries = float(model_width * model_width)
    square = gradient * gradient
    squares = square + tiny_term
    row_new = decay_rate * row_state[0] + (1.0 - decay_rate) * jnp.mean(squares, axis=1)
    col_part = jnp.sum(squares, axis=0)
    scaled_part = jnp.sum(square / row_new[:, None], axis=0)
    col_sum, scaled_sum, row_total, weight_total = lax.psum(
        (col_part, scaled_part, jnp.sum(row_new), jnp.sum(weight_float * weight_float)), "tensor"
    )
    col_new = decay_rate * col_state[0] + (1.0 - decay_rate) * (col_sum / model_width)
    update_total = row_total * jnp.sum(scaled_sum / col_new)
    factor = (
        learn_rate
        * jnp.sqrt(weight_total / entries)
        / jnp.maximum(1.0, jnp.sqrt(update_total / entries))
    )
    update = gradient * (lax.rsqrt(row_new)[:, None] * (lax.rsqrt(col_new) * jnp.sqrt(row_total))[None, :])
    new_weight = (weight_float - factor * update).astype(jnp.bfloat16)
    return (loss, outputs.T[None], new_weight[None], row_new[None], col_new[None])


def solution(mesh):
    return jax.shard_map(
        body,
        mesh=mesh,
        in_specs=(
            P(None, "tensor"),
            P(),
            P(None, "tensor"),
            P("section", None, "tensor"),
            P("section", "tensor", None),
            P("section", "tensor"),
            P("section", None),
        ),
        out_specs=(
            P(),
            P("section", None, "tensor"),
            P("section", "tensor", None),
            P("section", "tensor"),
            P("section", None),
        ),
        check_vma=False,
    )
```

```python
import functools

import jax
import jax.numpy as jnp
from jax import lax
from jax.experimental import pallas as pl
from jax.experimental.pallas import tpu as pltpu
from jax.sharding import PartitionSpec as P

decay_rate = 0.9
learn_rate = 0.3
tiny_term = 1e-30


MESH = pl.DeviceIdType.MESH


def chain_kernel(
    sections, tensors, part_ref, loss_ref, w_ref, out_ref, g_ref, total_ref, square_ref,
    acc_ref, loss_buf, send_x, recv_x, send_ring, recv_ring, send_mate, recv_mate, send_loss, recv_loss, head_sem,
):
    section = lax.axis_index("section")
    me = lax.axis_index("tensor")
    chips = tensors // 2
    chip, core = me // 2, me % 2
    right = lax.rem(chip + 1, chips) * 2 + core
    left = lax.rem(chip + chips - 1, chips) * 2 + core
    mate = chip * 2 + 1 - core
    features, lanes = part_ref.shape
    half = features // 2 // 16 * 16
    last = sections - 1
    reach = chips // 2

    def block(share, origin, low, size):
        rows = pl.ds(pl.multiple_of(origin * features + low, 16), size)
        return g_ref.at[rows, pl.ds(pl.multiple_of(share * lanes, lanes), lanes)]

    def span(way, distance):
        if 2 * distance < chips:
            return 0, features
        return (0, half) if way == 0 else (half, features - half)

    def remote(src, dst, send, recv, device):
        return pltpu.make_async_remote_copy(
            src_ref=src, dst_ref=dst, send_sem=send, recv_sem=recv, device_id=device, device_id_type=MESH
        )

    def origin_of(way, distance):
        there = chip - distance if way == 0 else chip + distance
        return lax.rem(there + chips, chips) * 2 + core

    def ring_copy(share, way, distance, origin):
        low, size = span(way, distance)
        where = block(share, origin, low, size)
        slot = (share, way * reach + distance - 1)
        return remote(
            where, where, send_ring.at[slot], recv_ring.at[slot], {"tensor": right if way == 0 else left}
        )

    def mate_copy(share, way, distance, origin):
        low, size = (0, features) if distance == 0 else span(way, distance)
        where = block(share, origin, low, size)
        slot = (share, 0 if distance == 0 else 1 + way * reach + distance - 1)
        return remote(where, where, send_mate.at[slot], recv_mate.at[slot], {"tensor": mate})

    def down_copy(share):
        columns = pl.ds(pl.multiple_of(share * lanes, lanes), lanes)
        below = jnp.maximum(section - 1, 0)
        return remote(
            out_ref.at[:, columns], block(share, me, 0, features),
            send_x.at[share], recv_x.at[share], {"section": below},
        )

    def head_copy():
        return remote(
            part_ref, block(section, me, 0, features), head_sem.at[0], recv_x.at[section], {"section": last}
        )

    def own_copy():
        return pltpu.make_async_copy(part_ref, block(last, me, 0, features), head_sem.at[1])

    def loss_copy(step):
        other = lax.rem(section + step, sections)
        return remote(
            loss_ref, loss_buf.at[step - 1], send_loss.at[step - 1], recv_loss.at[step - 1], {"section": other}
        )

    barrier = pltpu.get_barrier_semaphore()
    greeted = [{"tensor": mate}]
    if reach:
        greeted += [{"tensor": right}, {"tensor": left}]
    greeted += [{"section": lax.rem(section + step, sections)} for step in range(1, sections)]
    for device in greeted:
        pl.semaphore_signal(barrier, inc=1, device_id=device, device_id_type=MESH)
    pl.semaphore_wait(barrier, len(greeted))

    @pl.when(section == last)
    def _():
        own_copy().start()

    @pl.when(section != last)
    def _():
        head_copy().start()

    for step in range(1, sections):
        loss_copy(step).start()

    tile = features // 2 if features > 416 else features
    pair = 2 * features
    split = pair % 128 == 0

    def add_squares():
        def rows_step(index, inner):
            entries = w_ref[pl.ds(pl.multiple_of(index * 16, 16), 16), :].astype(jnp.float32)
            return inner + jnp.sum(jnp.reshape(entries * entries, (2, 8, entries.shape[1])), axis=0)

        width = w_ref.shape[1]
        sums = lax.fori_loop(0, features // 16, rows_step, jnp.zeros((8, width), jnp.float32))
        folded = sums[:, :128]
        for start in range(128, width, 128):
            folded = folded + sums[:, start : start + 128]
        square_ref[...] = folded

    @pl.when(section != last)
    def _():
        add_squares()

    def advance(share, carry):
        @pl.when((section == last) & (share == last))
        def _():
            own_copy().wait()

        @pl.when((section != last) | (share != last))
        def _():
            down_copy(share).wait_recv()

        if reach:
            ring_copy(share, 0, 1, me).start()
            ring_copy(share, 1, 1, me).start()
        mate_copy(share, 0, 0, me).start()
        columns = pl.ds(pl.multiple_of(share * lanes, lanes), lanes)
        other = 1 - 2 * core

        def product_of(owner_chip, first):
            if owner_chip is None:
                depth = slice(None)
            else:
                depth = pl.ds(pl.multiple_of(owner_chip * pair, 128), pair)

            def rows_step(index, inner):
                rows = pl.ds(pl.multiple_of(index * tile, 16), tile)
                product = jnp.dot(w_ref[rows, depth], g_ref[depth, columns], preferred_element_type=jnp.float32)
                acc_ref[rows, :] = product if first else acc_ref[rows, :] + product
                return inner

            lax.fori_loop(0, features // tile, rows_step, 0)

        mate_copy(share, 0, 0, me + other).wait_recv()
        if split:
            product_of(chip, True)
        for distance in range(1, reach + 1):
            for way in (0, 1):
                origin = origin_of(way, distance)
                ring_copy(share, way, distance, origin).wait_recv()
                if distance < reach:
                    ring_copy(share, way, distance + 1, origin).start()
                mate_copy(share, way, distance, origin).start()
            for way in (0, 1):
                mate_copy(share, way, distance, origin_of(way, distance) + other).wait_recv()
                if split and (way == 1 or 2 * distance < chips):
                    product_of(origin_of(way, distance) // 2, False)
        if not split:
            product_of(None, True)
        mine = g_ref[pl.ds(pl.multiple_of(me * features, 16), features), columns]
        out_ref[:, columns] = (mine.astype(jnp.float32) + acc_ref[...]).astype(out_ref.dtype)

        @pl.when(section > 0)
        def _():
            down_copy(share).start()

        return carry

    lax.fori_loop(0, sections, advance, 0)

    @pl.when(section == last)
    def _():
        add_squares()

    total = loss_ref[...]
    for step in range(1, sections):
        loss_copy(step).wait_recv()
        total = total + loss_buf[step - 1]
    total_ref[...] = total

    def finish(share, carry):
        @pl.when(section > 0)
        def _():
            down_copy(share).wait_send()

        if reach:
            ring_copy(share, 0, 1, me).wait_send()
            ring_copy(share, 1, 1, me).wait_send()
        mate_copy(share, 0, 0, me).wait_send()
        for distance in range(1, reach + 1):
            for way in (0, 1):
                origin = origin_of(way, distance)
                if distance < reach:
                    ring_copy(share, way, distance + 1, origin).wait_send()
                mate_copy(share, way, distance, origin).wait_send()
        return carry

    lax.fori_loop(0, sections, finish, 0)
    for step in range(1, sections):
        loss_copy(step).wait_send()

    @pl.when(section != last)
    def _():
        head_copy().wait_send()


def gather_kernel(tensors, x_ref, g_ref, send_ring, recv_ring, send_mate, recv_mate, own_sem):
    me = lax.axis_index("tensor")
    chips = tensors // 2
    chip, core = me // 2, me % 2
    right = lax.rem(chip + 1, chips) * 2 + core
    left = lax.rem(chip + chips - 1, chips) * 2 + core
    mate = chip * 2 + 1 - core
    features = x_ref.shape[0]
    half = features // 2 // 16 * 16
    reach = chips // 2

    barrier = pltpu.get_barrier_semaphore()
    greeted = [mate] + ([right, left] if reach else [])
    for device in greeted:
        pl.semaphore_signal(barrier, inc=1, device_id={"tensor": device}, device_id_type=MESH)
    pl.semaphore_wait(barrier, len(greeted))

    def copy(way, distance, origin, to_mate):
        low, size = 0, features
        if distance and 2 * distance == chips:
            low, size = (0, half) if way == 0 else (half, features - half)
        where = g_ref.at[pl.ds(pl.multiple_of(origin * features + low, 16), size), :]
        own = (distance == 0) if to_mate else (distance == 1)
        slot = 0 if distance == 0 else way * reach + distance - 1 + int(to_mate)
        send, recv = (send_mate, recv_mate) if to_mate else (send_ring, recv_ring)
        target = mate if to_mate else (right if way == 0 else left)
        return pltpu.make_async_remote_copy(
            src_ref=x_ref.at[pl.ds(low, size), :] if own else where, dst_ref=where,
            send_sem=send.at[slot], recv_sem=recv.at[slot],
            device_id={"tensor": target}, device_id_type=MESH,
        )

    def origin_of(way, distance):
        there = chip - distance if way == 0 else chip + distance
        return lax.rem(there + chips, chips) * 2 + core

    sent = []

    def start(*args):
        copy(*args).start()
        sent.append(args)

    own_block = g_ref.at[pl.ds(pl.multiple_of(me * features, 16), features), :]
    keep = pltpu.make_async_copy(x_ref, own_block, own_sem.at[0])
    if reach:
        start(0, 1, me, False)
        start(1, 1, me, False)
    start(0, 0, me, True)
    keep.start()
    for distance in range(1, reach + 1):
        for way in (0, 1):
            origin = origin_of(way, distance)
            copy(way, distance, origin, False).wait_recv()
            if distance < reach:
                start(way, distance + 1, origin, False)
            start(way, distance, origin, True)
    other = 1 - 2 * core
    copy(0, 0, me + other, True).wait_recv()
    for distance in range(1, reach + 1):
        for way in (0, 1):
            copy(way, distance, origin_of(way, distance) + other, True).wait_recv()
    keep.wait()
    for args in sent:
        copy(*args).wait_send()


def gather_rows(x, collective_id):
    tensors = lax.axis_size("tensor")
    ring = max(2 * (tensors // 4), 1)
    vmem = pl.BlockSpec(memory_space=pltpu.VMEM)
    dma = pltpu.SemaphoreType.DMA
    return pl.pallas_call(
        functools.partial(gather_kernel, tensors),
        out_shape=jax.ShapeDtypeStruct((tensors * x.shape[0], x.shape[1]), x.dtype),
        in_specs=[vmem],
        out_specs=vmem,
        scratch_shapes=[dma((ring,)), dma((ring,)), dma((ring + 1,)), dma((ring + 1,)), dma((1,))],
        compiler_params=pltpu.CompilerParams(
            collective_id=collective_id, has_side_effects=True, vmem_limit_bytes=24 * 1024 * 1024
        ),
    )(x)


def scatter_kernel(tensors, x_ref, out_ref, near, stage, far, send_near, recv_near, send_far, recv_far):
    me = lax.axis_index("tensor")
    chips = tensors // 2
    chip, core = me // 2, me % 2
    mate = chip * 2 + 1 - core
    features = out_ref.shape[0]

    barrier = pltpu.get_barrier_semaphore()
    chips_out = [lax.rem(chip + step, chips) for step in range(1, chips)]
    greeted = [mate] + [there * 2 + core for there in chips_out]
    for device in greeted:
        pl.semaphore_signal(barrier, inc=1, device_id={"tensor": device}, device_id_type=MESH)
    pl.semaphore_wait(barrier, len(greeted))

    def rows_of(device):
        return pl.ds(pl.multiple_of(device * features, 16), features)

    def near_copy(there):
        return pltpu.make_async_remote_copy(
            src_ref=x_ref.at[rows_of(there * 2 + 1 - core), :], dst_ref=near.at[there],
            send_sem=send_near.at[there], recv_sem=recv_near.at[there],
            device_id={"tensor": mate}, device_id_type=MESH,
        )

    def far_copy(source, there):
        return pltpu.make_async_remote_copy(
            src_ref=stage.at[there], dst_ref=far.at[source],
            send_sem=send_far.at[there], recv_sem=recv_far.at[source],
            device_id={"tensor": there * 2 + core}, device_id_type=MESH,
        )

    def pair_sum(there):
        near_copy(there).wait_recv()
        mine = x_ref[rows_of(there * 2 + core), :].astype(jnp.float32)
        return mine + near[there].astype(jnp.float32)

    for there in chips_out + [chip]:
        near_copy(there).start()
    for there in chips_out:
        stage[there] = pair_sum(there).astype(stage.dtype)
        far_copy(chip, there).start()
    total = pair_sum(chip)
    for there in chips_out:
        far_copy(there, there).wait_recv()
        total = total + far[there].astype(jnp.float32)
    out_ref[...] = total.astype(out_ref.dtype)
    for there in chips_out + [chip]:
        near_copy(there).wait_send()
    for there in chips_out:
        far_copy(chip, there).wait_send()


def scatter_rows(x, collective_id):
    tensors = lax.axis_size("tensor")
    chips = tensors // 2
    features = x.shape[0] // tensors
    vmem = pl.BlockSpec(memory_space=pltpu.VMEM)
    dma = pltpu.SemaphoreType.DMA
    held = pltpu.VMEM((chips, features, x.shape[1]), x.dtype)
    return pl.pallas_call(
        functools.partial(scatter_kernel, tensors),
        out_shape=jax.ShapeDtypeStruct((features, x.shape[1]), x.dtype),
        in_specs=[vmem],
        out_specs=vmem,
        scratch_shapes=[held, held, held] + [dma((chips,))] * 4,
        compiler_params=pltpu.CompilerParams(
            collective_id=collective_id, has_side_effects=True, vmem_limit_bytes=24 * 1024 * 1024
        ),
    )(x)


def exchange_kernel(tensors, x_ref, out_ref, held, send, recv):
    me = lax.axis_index("tensor")
    barrier = pltpu.get_barrier_semaphore()
    others = [lax.rem(me + step, tensors) for step in range(1, tensors)]
    for other in others:
        pl.semaphore_signal(barrier, inc=1, device_id={"tensor": other}, device_id_type=MESH)
    pl.semaphore_wait(barrier, tensors - 1)

    def copy(source, other):
        return pltpu.make_async_remote_copy(
            src_ref=x_ref, dst_ref=held.at[source], send_sem=send.at[other], recv_sem=recv.at[source],
            device_id={"tensor": other}, device_id_type=MESH,
        )

    for other in others:
        copy(me, other).start()
    held[me] = x_ref[...]
    for other in others:
        copy(other, other).wait_recv()
    out_ref[...] = jnp.sum(held[...], axis=0)
    for other in others:
        copy(me, other).wait_send()


def exchange(x, collective_id):
    tensors = lax.axis_size("tensor")
    vmem = pl.BlockSpec(memory_space=pltpu.VMEM)
    dma = pltpu.SemaphoreType.DMA
    return pl.pallas_call(
        functools.partial(exchange_kernel, tensors),
        out_shape=jax.ShapeDtypeStruct(x.shape, x.dtype),
        in_specs=[vmem],
        out_specs=vmem,
        scratch_shapes=[pltpu.VMEM((tensors,) + x.shape, x.dtype), dma((tensors,)), dma((tensors,))],
        compiler_params=pltpu.CompilerParams(
            collective_id=collective_id, has_side_effects=True, vmem_limit_bytes=24 * 1024 * 1024
        ),
    )(x)


def packed_sum(parts, collective_id):
    flat = jnp.concatenate([jnp.reshape(part, (-1,)) for part in parts])
    rows = -(-flat.shape[0] // 1024) * 8
    flat = jnp.pad(flat, (0, rows * 128 - flat.shape[0])).reshape(rows, 128)
    flat = exchange(flat, collective_id).reshape(-1)
    sums, start = [], 0
    for part in parts:
        sums.append(flat[start : start + part.size].reshape(part.shape))
        start += part.size
    return sums


def chain(part_grad, part_loss, local_weight):
    sections, tensors = lax.axis_size("section"), lax.axis_size("tensor")
    features, lanes = part_grad.shape
    width = features * tensors
    rows = lanes * sections
    ring = max(2 * (tensors // 4), 1)
    dma = pltpu.SemaphoreType.DMA
    vmem = pl.BlockSpec(memory_space=pltpu.VMEM)
    return pl.pallas_call(
        functools.partial(chain_kernel, sections, tensors),
        out_shape=(
            jax.ShapeDtypeStruct((features, rows), jnp.bfloat16),
            jax.ShapeDtypeStruct((width, rows), jnp.bfloat16),
            jax.ShapeDtypeStruct((8, 128), jnp.float32),
            jax.ShapeDtypeStruct((8, 128), jnp.float32),
        ),
        in_specs=[vmem] * 3,
        out_specs=(vmem, vmem, vmem, vmem),
        scratch_shapes=[
            pltpu.VMEM((features, lanes), jnp.float32),
            pltpu.VMEM((max(sections - 1, 1), 8, 128), jnp.float32),
            dma((sections,)),
            dma((sections,)),
            dma((sections, ring)),
            dma((sections, ring)),
            dma((sections, ring + 1)),
            dma((sections, ring + 1)),
            dma((max(sections - 1, 1),)),
            dma((max(sections - 1, 1),)),
            dma((2,)),
        ],
        compiler_params=pltpu.CompilerParams(
            collective_id=0, has_side_effects=True, vmem_limit_bytes=48 * 1024 * 1024
        ),
    )(part_grad, jnp.full((8, 128), part_loss, jnp.float32), local_weight)


def body(hidden_last, labels, head_weight, layer_inputs, weights, row_state, col_state):
    section_count = lax.axis_size("section")
    section_index = lax.axis_index("section")
    all_rows = labels.shape[0]
    model_width = head_weight.shape[0]
    vocab_local = head_weight.shape[1]
    local_weight = weights[0]
    rows_local = local_weight.shape[0]
    saved_all = layer_inputs[0]
    columns = lax.axis_index("tensor") * vocab_local + lax.iota(jnp.int32, vocab_local)
    share_rows = all_rows // section_count
    row_start = section_index * share_rows
    hidden_rows = lax.dynamic_slice_in_dim(hidden_last, row_start, share_rows, 0)
    head_slice = head_weight
    logits = lax.dot_general(
        gather_rows(hidden_rows.T, 3),
        head_slice,
        (((0,), (0,)), ((), ())),
        preferred_element_type=jnp.float32,
    )
    exponent = jnp.exp(logits)
    label_hit = (
        lax.dynamic_slice_in_dim(labels, row_start, share_rows, 0)[:, None] == columns[None, :]
    )
    denominator, picked = packed_sum(
        (
            jnp.sum(exponent, axis=1),
            jnp.sum(jnp.where(label_hit, logits, jnp.zeros_like(logits)), axis=1),
        ),
        1,
    )
    losses = jnp.log(denominator) - picked
    logit_grad = (
        (exponent / denominator[:, None] - label_hit.astype(jnp.float32)) / all_rows
    ).astype(jnp.bfloat16)
    head_slice = head_weight
    part_grad = scatter_rows(
        lax.dot_general(
            head_slice, logit_grad, (((1,), (1,)), ((), ())), preferred_element_type=jnp.float32
        ).astype(jnp.bfloat16),
        4,
    )
    part_loss = jnp.sum(losses)
    outputs, gathered, total, weight_squares = chain(part_grad, part_loss, local_weight)
    loss = total[0, 0] / all_rows
    gradient = lax.dot_general(
        saved_all, gathered, (((0,), (1,)), ((), ())), preferred_element_type=jnp.float32
    )
    weight_float = local_weight.astype(jnp.float32)
    entries = float(model_width * model_width)
    square = gradient * gradient
    squares = square + tiny_term
    row_new = decay_rate * row_state[0] + (1.0 - decay_rate) * jnp.mean(squares, axis=1)
    col_part = jnp.sum(squares, axis=0)
    scaled_part = jnp.sum(square / row_new[:, None], axis=0)
    col_sum, scaled_sum, row_total, weight_total = packed_sum(
        (col_part, scaled_part, jnp.sum(row_new), jnp.sum(weight_squares)), 2
    )
    col_new = decay_rate * col_state[0] + (1.0 - decay_rate) * (col_sum / model_width)
    update_total = row_total * jnp.sum(scaled_sum / col_new)
    factor = (
        learn_rate
        * jnp.sqrt(weight_total / entries)
        / jnp.maximum(1.0, jnp.sqrt(update_total / entries))
    )
    update = gradient * (lax.rsqrt(row_new)[:, None] * (lax.rsqrt(col_new) * jnp.sqrt(row_total))[None, :])
    new_weight = (weight_float - factor * update).astype(jnp.bfloat16)
    return (loss, outputs.T[None], new_weight[None], row_new[None], col_new[None])


def solution(mesh):
    return jax.shard_map(
        body,
        mesh=mesh,
        in_specs=(
            P(None, "tensor"),
            P(),
            P(None, "tensor"),
            P("section", None, "tensor"),
            P("section", "tensor", None),
            P("section", "tensor"),
            P("section", None),
        ),
        out_specs=(
            P(),
            P("section", None, "tensor"),
            P("section", "tensor", None),
            P("section", "tensor"),
            P("section", None),
        ),
        check_vma=False,
    )
```

```python
import functools

import jax
import jax.numpy as jnp
from jax import lax
from jax.experimental import pallas as pl
from jax.experimental.pallas import tpu as pltpu
from jax.sharding import PartitionSpec as P

decay_rate = 0.9
learn_rate = 0.3
tiny_term = 1e-30


MESH = pl.DeviceIdType.MESH


def chain_kernel(
    sections, tensors, part_ref, loss_ref, w_ref, out_ref, g_ref, total_ref, square_ref,
    acc_ref, loss_buf, send_x, recv_x, send_ring, recv_ring, send_mate, recv_mate, send_loss, recv_loss, head_sem,
):
    section = lax.axis_index("section")
    me = lax.axis_index("tensor")
    chips = tensors // 2
    chip, core = me // 2, me % 2
    right = lax.rem(chip + 1, chips) * 2 + core
    left = lax.rem(chip + chips - 1, chips) * 2 + core
    mate = chip * 2 + 1 - core
    features, lanes = part_ref.shape
    half = features // 2 // 16 * 16
    last = sections - 1
    reach = chips // 2

    def block(share, origin, low, size):
        rows = pl.ds(pl.multiple_of(origin * features + low, 16), size)
        return g_ref.at[rows, pl.ds(pl.multiple_of(share * lanes, lanes), lanes)]

    def span(way, distance):
        if 2 * distance < chips:
            return 0, features
        return (0, half) if way == 0 else (half, features - half)

    def remote(src, dst, send, recv, device):
        return pltpu.make_async_remote_copy(
            src_ref=src, dst_ref=dst, send_sem=send, recv_sem=recv, device_id=device, device_id_type=MESH
        )

    def origin_of(way, distance):
        there = chip - distance if way == 0 else chip + distance
        return lax.rem(there + chips, chips) * 2 + core

    def ring_copy(share, way, distance, origin):
        low, size = span(way, distance)
        where = block(share, origin, low, size)
        slot = (share, way * reach + distance - 1)
        return remote(
            where, where, send_ring.at[slot], recv_ring.at[slot], {"tensor": right if way == 0 else left}
        )

    def mate_copy(share, way, distance, origin):
        low, size = (0, features) if distance == 0 else span(way, distance)
        where = block(share, origin, low, size)
        slot = (share, 0 if distance == 0 else 1 + way * reach + distance - 1)
        return remote(where, where, send_mate.at[slot], recv_mate.at[slot], {"tensor": mate})

    def down_copy(share):
        columns = pl.ds(pl.multiple_of(share * lanes, lanes), lanes)
        below = jnp.maximum(section - 1, 0)
        return remote(
            out_ref.at[:, columns], block(share, me, 0, features),
            send_x.at[share], recv_x.at[share], {"section": below},
        )

    def head_copy():
        return remote(
            part_ref, block(section, me, 0, features), head_sem.at[0], recv_x.at[section], {"section": last}
        )

    def own_copy():
        return pltpu.make_async_copy(part_ref, block(last, me, 0, features), head_sem.at[1])

    def loss_copy(step):
        other = lax.rem(section + step, sections)
        return remote(
            loss_ref, loss_buf.at[step - 1], send_loss.at[step - 1], recv_loss.at[step - 1], {"section": other}
        )

    barrier = pltpu.get_barrier_semaphore()
    greeted = [{"tensor": mate}]
    if reach:
        greeted += [{"tensor": right}, {"tensor": left}]
    greeted += [{"section": lax.rem(section + step, sections)} for step in range(1, sections)]
    for device in greeted:
        pl.semaphore_signal(barrier, inc=1, device_id=device, device_id_type=MESH)
    pl.semaphore_wait(barrier, len(greeted))

    @pl.when(section == last)
    def _():
        own_copy().start()

    @pl.when(section != last)
    def _():
        head_copy().start()

    for step in range(1, sections):
        loss_copy(step).start()

    tile = features // 2 if features > 416 else features
    pair = 2 * features
    split = pair % 128 == 0

    def add_squares():
        def rows_step(index, inner):
            entries = w_ref[pl.ds(pl.multiple_of(index * 16, 16), 16), :].astype(jnp.float32)
            return inner + jnp.sum(jnp.reshape(entries * entries, (2, 8, entries.shape[1])), axis=0)

        width = w_ref.shape[1]
        sums = lax.fori_loop(0, features // 16, rows_step, jnp.zeros((8, width), jnp.float32))
        folded = sums[:, :128]
        for start in range(128, width, 128):
            folded = folded + sums[:, start : start + 128]
        square_ref[...] = folded

    @pl.when(section != last)
    def _():
        add_squares()

    def begin(share):
        @pl.when((section == last) & (share == last))
        def _():
            own_copy().wait()

        @pl.when((section != last) | (share != last))
        def _():
            down_copy(share).wait_recv()

        if reach:
            ring_copy(share, 0, 1, me).start()
            ring_copy(share, 1, 1, me).start()
        mate_copy(share, 0, 0, me).start()

    def advance(share, carry):
        columns = pl.ds(pl.multiple_of(share * lanes, lanes), lanes)
        other = 1 - 2 * core

        def begin_next():
            @pl.when(share < last)
            def _():
                begin(share + 1)

        def product_of(owner_chip, first):
            if owner_chip is None:
                depth = slice(None)
            else:
                depth = pl.ds(pl.multiple_of(owner_chip * pair, 128), pair)

            def rows_step(index, inner):
                rows = pl.ds(pl.multiple_of(index * tile, 16), tile)
                product = jnp.dot(w_ref[rows, depth], g_ref[depth, columns], preferred_element_type=jnp.float32)
                acc_ref[rows, :] = product if first else acc_ref[rows, :] + product
                return inner

            lax.fori_loop(0, features // tile, rows_step, 0)

        mate_copy(share, 0, 0, me + other).wait_recv()
        if split:
            product_of(chip, True)
        for distance in range(1, reach + 1):
            for way in (0, 1):
                origin = origin_of(way, distance)
                ring_copy(share, way, distance, origin).wait_recv()
                if distance < reach:
                    ring_copy(share, way, distance + 1, origin).start()
                mate_copy(share, way, distance, origin).start()
            for way in (0, 1):
                mate_copy(share, way, distance, origin_of(way, distance) + other).wait_recv()
                if distance == reach and way == 1:
                    begin_next()
                if split and (way == 1 or 2 * distance < chips):
                    product_of(origin_of(way, distance) // 2, False)
        if not reach:
            begin_next()
        if not split:
            product_of(None, True)
        mine = g_ref[pl.ds(pl.multiple_of(me * features, 16), features), columns]
        out_ref[:, columns] = (mine.astype(jnp.float32) + acc_ref[...]).astype(out_ref.dtype)

        @pl.when(section > 0)
        def _():
            down_copy(share).start()

        return carry

    begin(0)
    lax.fori_loop(0, sections, advance, 0)

    @pl.when(section == last)
    def _():
        add_squares()

    total = loss_ref[...]
    for step in range(1, sections):
        loss_copy(step).wait_recv()
        total = total + loss_buf[step - 1]
    total_ref[...] = total

    def finish(share, carry):
        @pl.when(section > 0)
        def _():
            down_copy(share).wait_send()

        if reach:
            ring_copy(share, 0, 1, me).wait_send()
            ring_copy(share, 1, 1, me).wait_send()
        mate_copy(share, 0, 0, me).wait_send()
        for distance in range(1, reach + 1):
            for way in (0, 1):
                origin = origin_of(way, distance)
                if distance < reach:
                    ring_copy(share, way, distance + 1, origin).wait_send()
                mate_copy(share, way, distance, origin).wait_send()
        return carry

    lax.fori_loop(0, sections, finish, 0)
    for step in range(1, sections):
        loss_copy(step).wait_send()

    @pl.when(section != last)
    def _():
        head_copy().wait_send()


def gather_kernel(tensors, x_ref, g_ref, send_ring, recv_ring, send_mate, recv_mate, own_sem):
    me = lax.axis_index("tensor")
    chips = tensors // 2
    chip, core = me // 2, me % 2
    right = lax.rem(chip + 1, chips) * 2 + core
    left = lax.rem(chip + chips - 1, chips) * 2 + core
    mate = chip * 2 + 1 - core
    features = x_ref.shape[0]
    half = features // 2 // 16 * 16
    reach = chips // 2

    barrier = pltpu.get_barrier_semaphore()
    greeted = [mate] + ([right, left] if reach else [])
    for device in greeted:
        pl.semaphore_signal(barrier, inc=1, device_id={"tensor": device}, device_id_type=MESH)
    pl.semaphore_wait(barrier, len(greeted))

    def copy(way, distance, origin, to_mate):
        low, size = 0, features
        if distance and 2 * distance == chips:
            low, size = (0, half) if way == 0 else (half, features - half)
        where = g_ref.at[pl.ds(pl.multiple_of(origin * features + low, 16), size), :]
        own = (distance == 0) if to_mate else (distance == 1)
        slot = 0 if distance == 0 else way * reach + distance - 1 + int(to_mate)
        send, recv = (send_mate, recv_mate) if to_mate else (send_ring, recv_ring)
        target = mate if to_mate else (right if way == 0 else left)
        return pltpu.make_async_remote_copy(
            src_ref=x_ref.at[pl.ds(low, size), :] if own else where, dst_ref=where,
            send_sem=send.at[slot], recv_sem=recv.at[slot],
            device_id={"tensor": target}, device_id_type=MESH,
        )

    def origin_of(way, distance):
        there = chip - distance if way == 0 else chip + distance
        return lax.rem(there + chips, chips) * 2 + core

    sent = []

    def start(*args):
        copy(*args).start()
        sent.append(args)

    own_block = g_ref.at[pl.ds(pl.multiple_of(me * features, 16), features), :]
    keep = pltpu.make_async_copy(x_ref, own_block, own_sem.at[0])
    if reach:
        start(0, 1, me, False)
        start(1, 1, me, False)
    start(0, 0, me, True)
    keep.start()
    for distance in range(1, reach + 1):
        for way in (0, 1):
            origin = origin_of(way, distance)
            copy(way, distance, origin, False).wait_recv()
            if distance < reach:
                start(way, distance + 1, origin, False)
            start(way, distance, origin, True)
    other = 1 - 2 * core
    copy(0, 0, me + other, True).wait_recv()
    for distance in range(1, reach + 1):
        for way in (0, 1):
            copy(way, distance, origin_of(way, distance) + other, True).wait_recv()
    keep.wait()
    for args in sent:
        copy(*args).wait_send()


def gather_rows(x, collective_id):
    tensors = lax.axis_size("tensor")
    ring = max(2 * (tensors // 4), 1)
    vmem = pl.BlockSpec(memory_space=pltpu.VMEM)
    dma = pltpu.SemaphoreType.DMA
    return pl.pallas_call(
        functools.partial(gather_kernel, tensors),
        out_shape=jax.ShapeDtypeStruct((tensors * x.shape[0], x.shape[1]), x.dtype),
        in_specs=[vmem],
        out_specs=vmem,
        scratch_shapes=[dma((ring,)), dma((ring,)), dma((ring + 1,)), dma((ring + 1,)), dma((1,))],
        compiler_params=pltpu.CompilerParams(
            collective_id=collective_id, has_side_effects=True, vmem_limit_bytes=24 * 1024 * 1024
        ),
    )(x)


def scatter_kernel(tensors, x_ref, out_ref, near, stage, far, send_near, recv_near, send_far, recv_far):
    me = lax.axis_index("tensor")
    chips = tensors // 2
    chip, core = me // 2, me % 2
    mate = chip * 2 + 1 - core
    features = out_ref.shape[0]

    barrier = pltpu.get_barrier_semaphore()
    chips_out = [lax.rem(chip + step, chips) for step in range(1, chips)]
    greeted = [mate] + [there * 2 + core for there in chips_out]
    for device in greeted:
        pl.semaphore_signal(barrier, inc=1, device_id={"tensor": device}, device_id_type=MESH)
    pl.semaphore_wait(barrier, len(greeted))

    def rows_of(device):
        return pl.ds(pl.multiple_of(device * features, 16), features)

    def near_copy(there):
        return pltpu.make_async_remote_copy(
            src_ref=x_ref.at[rows_of(there * 2 + 1 - core), :], dst_ref=near.at[there],
            send_sem=send_near.at[there], recv_sem=recv_near.at[there],
            device_id={"tensor": mate}, device_id_type=MESH,
        )

    def far_copy(source, there):
        return pltpu.make_async_remote_copy(
            src_ref=stage.at[there], dst_ref=far.at[source],
            send_sem=send_far.at[there], recv_sem=recv_far.at[source],
            device_id={"tensor": there * 2 + core}, device_id_type=MESH,
        )

    def pair_sum(there):
        near_copy(there).wait_recv()
        return x_ref[rows_of(there * 2 + core), :] + near[there]

    for there in chips_out + [chip]:
        near_copy(there).start()
    for there in chips_out:
        stage[there] = pair_sum(there).astype(stage.dtype)
        far_copy(chip, there).start()
    total = pair_sum(chip)
    for there in chips_out:
        far_copy(there, there).wait_recv()
        total = total + far[there].astype(jnp.float32)
    out_ref[...] = total.astype(out_ref.dtype)
    for there in chips_out + [chip]:
        near_copy(there).wait_send()
    for there in chips_out:
        far_copy(chip, there).wait_send()


def scatter_rows(x, collective_id):
    tensors = lax.axis_size("tensor")
    chips = tensors // 2
    features = x.shape[0] // tensors
    vmem = pl.BlockSpec(memory_space=pltpu.VMEM)
    dma = pltpu.SemaphoreType.DMA
    held = pltpu.VMEM((chips, features, x.shape[1]), jnp.bfloat16)
    return pl.pallas_call(
        functools.partial(scatter_kernel, tensors),
        out_shape=jax.ShapeDtypeStruct((features, x.shape[1]), jnp.bfloat16),
        in_specs=[vmem],
        out_specs=vmem,
        scratch_shapes=[pltpu.VMEM((chips, features, x.shape[1]), x.dtype), held, held] + [dma((chips,))] * 4,
        compiler_params=pltpu.CompilerParams(
            collective_id=collective_id, has_side_effects=True, vmem_limit_bytes=24 * 1024 * 1024
        ),
    )(x)


def exchange_kernel(tensors, x_ref, out_ref, held, send, recv):
    me = lax.axis_index("tensor")
    barrier = pltpu.get_barrier_semaphore()
    others = [lax.rem(me + step, tensors) for step in range(1, tensors)]
    for other in others:
        pl.semaphore_signal(barrier, inc=1, device_id={"tensor": other}, device_id_type=MESH)
    pl.semaphore_wait(barrier, tensors - 1)

    def copy(source, other):
        return pltpu.make_async_remote_copy(
            src_ref=x_ref, dst_ref=held.at[source], send_sem=send.at[other], recv_sem=recv.at[source],
            device_id={"tensor": other}, device_id_type=MESH,
        )

    for other in others:
        copy(me, other).start()
    held[me] = x_ref[...]
    for other in others:
        copy(other, other).wait_recv()
    out_ref[...] = jnp.sum(held[...], axis=0)
    for other in others:
        copy(me, other).wait_send()


def exchange(x, collective_id):
    tensors = lax.axis_size("tensor")
    vmem = pl.BlockSpec(memory_space=pltpu.VMEM)
    dma = pltpu.SemaphoreType.DMA
    return pl.pallas_call(
        functools.partial(exchange_kernel, tensors),
        out_shape=jax.ShapeDtypeStruct(x.shape, x.dtype),
        in_specs=[vmem],
        out_specs=vmem,
        scratch_shapes=[pltpu.VMEM((tensors,) + x.shape, x.dtype), dma((tensors,)), dma((tensors,))],
        compiler_params=pltpu.CompilerParams(
            collective_id=collective_id, has_side_effects=True, vmem_limit_bytes=24 * 1024 * 1024
        ),
    )(x)


def packed_sum(parts, collective_id):
    flat = jnp.concatenate([jnp.reshape(part, (-1,)) for part in parts])
    rows = -(-flat.shape[0] // 1024) * 8
    flat = jnp.pad(flat, (0, rows * 128 - flat.shape[0])).reshape(rows, 128)
    flat = exchange(flat, collective_id).reshape(-1)
    sums, start = [], 0
    for part in parts:
        sums.append(flat[start : start + part.size].reshape(part.shape))
        start += part.size
    return sums


def chain(part_grad, part_loss, local_weight):
    sections, tensors = lax.axis_size("section"), lax.axis_size("tensor")
    features, lanes = part_grad.shape
    width = features * tensors
    rows = lanes * sections
    ring = max(2 * (tensors // 4), 1)
    dma = pltpu.SemaphoreType.DMA
    vmem = pl.BlockSpec(memory_space=pltpu.VMEM)
    return pl.pallas_call(
        functools.partial(chain_kernel, sections, tensors),
        out_shape=(
            jax.ShapeDtypeStruct((features, rows), jnp.bfloat16),
            jax.ShapeDtypeStruct((width, rows), jnp.bfloat16),
            jax.ShapeDtypeStruct((8, 128), jnp.float32),
            jax.ShapeDtypeStruct((8, 128), jnp.float32),
        ),
        in_specs=[vmem] * 3,
        out_specs=(vmem, vmem, vmem, vmem),
        scratch_shapes=[
            pltpu.VMEM((features, lanes), jnp.float32),
            pltpu.VMEM((max(sections - 1, 1), 8, 128), jnp.float32),
            dma((sections,)),
            dma((sections,)),
            dma((sections, ring)),
            dma((sections, ring)),
            dma((sections, ring + 1)),
            dma((sections, ring + 1)),
            dma((max(sections - 1, 1),)),
            dma((max(sections - 1, 1),)),
            dma((2,)),
        ],
        compiler_params=pltpu.CompilerParams(
            collective_id=0, has_side_effects=True, vmem_limit_bytes=48 * 1024 * 1024
        ),
    )(part_grad, jnp.full((8, 128), part_loss, jnp.float32), local_weight)


def body(hidden_last, labels, head_weight, layer_inputs, weights, row_state, col_state):
    section_count = lax.axis_size("section")
    section_index = lax.axis_index("section")
    all_rows = labels.shape[0]
    model_width = head_weight.shape[0]
    vocab_local = head_weight.shape[1]
    local_weight = weights[0]
    rows_local = local_weight.shape[0]
    saved_all = layer_inputs[0]
    columns = lax.axis_index("tensor") * vocab_local + lax.iota(jnp.int32, vocab_local)
    share_rows = all_rows // section_count
    row_start = section_index * share_rows
    hidden_rows = lax.dynamic_slice_in_dim(hidden_last, row_start, share_rows, 0)
    head_slice = head_weight
    logits = lax.dot_general(
        gather_rows(hidden_rows.T, 3),
        head_slice,
        (((0,), (0,)), ((), ())),
        preferred_element_type=jnp.float32,
    )
    exponent = jnp.exp(logits)
    label_hit = (
        lax.dynamic_slice_in_dim(labels, row_start, share_rows, 0)[:, None] == columns[None, :]
    )
    denominator, picked = packed_sum(
        (
            jnp.sum(exponent, axis=1),
            jnp.sum(jnp.where(label_hit, logits, jnp.zeros_like(logits)), axis=1),
        ),
        1,
    )
    losses = jnp.log(denominator) - picked
    logit_grad = (
        (exponent / denominator[:, None] - label_hit.astype(jnp.float32)) / all_rows
    ).astype(jnp.bfloat16)
    head_slice = head_weight
    part_grad = scatter_rows(
        lax.dot_general(
            head_slice, logit_grad, (((1,), (1,)), ((), ())), preferred_element_type=jnp.float32
        ),
        4,
    )
    part_loss = jnp.sum(losses)
    outputs, gathered, total, weight_squares = chain(part_grad, part_loss, local_weight)
    loss = total[0, 0] / all_rows
    gradient = lax.dot_general(
        saved_all, gathered, (((0,), (1,)), ((), ())), preferred_element_type=jnp.float32
    )
    weight_float = local_weight.astype(jnp.float32)
    entries = float(model_width * model_width)
    square = gradient * gradient
    squares = square + tiny_term
    row_new = decay_rate * row_state[0] + (1.0 - decay_rate) * jnp.mean(squares, axis=1)
    col_part = jnp.sum(squares, axis=0)
    scaled_part = jnp.sum(square / row_new[:, None], axis=0)
    col_sum, scaled_sum, row_total, weight_total = packed_sum(
        (col_part, scaled_part, jnp.sum(row_new), jnp.sum(weight_squares)), 2
    )
    col_new = decay_rate * col_state[0] + (1.0 - decay_rate) * (col_sum / model_width)
    update_total = row_total * jnp.sum(scaled_sum / col_new)
    factor = (
        learn_rate
        * jnp.sqrt(weight_total / entries)
        / jnp.maximum(1.0, jnp.sqrt(update_total / entries))
    )
    update = gradient * (lax.rsqrt(row_new)[:, None] * (lax.rsqrt(col_new) * jnp.sqrt(row_total))[None, :])
    new_weight = (weight_float - factor * update).astype(jnp.bfloat16)
    return (loss, outputs.T[None], new_weight[None], row_new[None], col_new[None])


def solution(mesh):
    return jax.shard_map(
        body,
        mesh=mesh,
        in_specs=(
            P(None, "tensor"),
            P(),
            P(None, "tensor"),
            P("section", None, "tensor"),
            P("section", "tensor", None),
            P("section", "tensor"),
            P("section", None),
        ),
        out_specs=(
            P(),
            P("section", None, "tensor"),
            P("section", "tensor", None),
            P("section", "tensor"),
            P("section", None),
        ),
        check_vma=False,
    )
```
